32 devices in a mesh: fsdp: 4 (over x, core), ctx: 4 (over z), tp: 2 (over y).
Axes of the slice: x: 2, y: 2, z: 4, core: 2. Of those that a mesh axis runs over, the one named last changes fastest.
Arguments:
- hidden_in: bfloat16 [1024, 4, 2048], P('ctx', 'fsdp', 'tp'), may hold values from -13 to 13
- out_grad: bfloat16 [1024, 4, 2048], P('ctx', 'fsdp', 'tp'), may hold values from -6 to 6
- segment_ids: int32 [4, 1024], P('fsdp'), may hold values from 0 to 7, as said below
- positions: int32 [4, 1024], P('fsdp'), may hold values from 0 to 1023, as said below
- ln_gain: bfloat16 [2048], replicated, may hold values from 0.099609375 to 1.8984375
- ln_bias: bfloat16 [2048], replicated, may hold values from -3 to 3
- w_qkv: bfloat16 [2048, 3, 2048], P(('fsdp', 'ctx'), None, 'tp'), may hold values from -2 to 2
- qkv_bias: bfloat16 [3, 2048], P(None, 'tp'), may hold values from -3 to 3
- w_out: bfloat16 [2048, 2048], P(('fsdp', 'ctx'), 'tp'), may hold values from -0.5 to 0.5
- w_up: bfloat16 [2048, 8192], P(('fsdp', 'ctx'), 'tp'), may hold values from -0.125 to 0.125
- up_bias: bfloat16 [8192], P('tp'), may hold values from -3 to 3
- w_down: bfloat16 [2048, 8192], P(('fsdp', 'ctx'), 'tp'), may hold values from -0.0625 to 0.0625
- out_bias: bfloat16 [2048], P('tp'), may hold values from -3 to 3
Outputs:
- block_out: bfloat16 [1024, 4, 2048], P('ctx', 'fsdp', 'tp')
- input_grad: float32 [1024, 4, 2048], P('ctx', 'fsdp', 'tp')
- ln_gain_grad: float32 [2048], P('tp')
- ln_bias_grad: float32 [2048], P('tp')
- qkv_grad: float32 [2048, 3, 2048], P(('fsdp', 'ctx'), None, 'tp')
- qkv_bias_grad: float32 [3, 2048], P(None, 'tp')
- out_weight_grad: float32 [2048, 2048], P(('fsdp', 'ctx'), 'tp')
- up_grad: float32 [2048, 8192], P(('fsdp', 'ctx'), 'tp')
- up_bias_grad: float32 [8192], P('tp')
- down_grad: float32 [2048, 8192], P(('fsdp', 'ctx'), 'tp')
- out_bias_grad: float32 [2048], P('tp')
The draws below stay inside these ranges and needn't reach their ends.
Inputs may be any that keep to these rules, and one draw needn't show every extreme that they name: `segment_ids`: along each row the ids start at 0 and rise by one at the first token of each document; every row but the last holds exactly 8 documents, the last row a single one. `positions`: each token's position counts from 0 at the first token of its document, with documents as the segment ids mark them.
All inputs are finite; a program needn't handle non-finite values.
Results may differ from the reference program's by a relative error of at most 0.03.
Values may be sent and summed in bfloat16 or wider, within the bound.
No kernel may reach another device: no remote copies, remote signals or barrier semaphores. Data moves between devices by JAX's collectives and lax.ppermute only.
A program may use at most 384 MiB of HBM per device.

```python
import math
import jax
import jax.numpy as jnp
from jax import lax

D = 2048
HEADS = 32
HD = 64
ROT = 32
FF = 8192
LEN = 1024
BATCH = 4


def draw_hidden_in(key, part):
    base_key = jax.random.fold_in(key, 21)
    key_rows, key_cols, key_vals = jax.random.split(base_key, 3)
    row_scale = jnp.exp(jax.random.uniform(key_rows, (LEN, BATCH, 1), jnp.float32, math.log(0.5), math.log(2.0)))
    col_scale = jnp.exp(jax.random.uniform(key_cols, (1, 1, D), jnp.float32, math.log(0.25), math.log(2.5)))
    values = jax.random.truncated_normal(key_vals, -2.5, 2.5, (LEN, BATCH, D), jnp.float32) * row_scale * col_scale
    return values.astype(jnp.bfloat16)


def draw_w_qkv(key, part):
    key_vals = jax.random.fold_in(key, 41)
    spread = 1.0 / math.sqrt(D)
    values = jax.random.truncated_normal(key_vals, -3.0, 3.0, (D, 3, D), jnp.float32) * spread
    return values.astype(jnp.bfloat16)


def document_layout(key):
    index_all = jnp.arange(LEN, dtype=jnp.int32)[None, :]
    row_index = jnp.arange(BATCH, dtype=jnp.int32)[:, None]
    row_keys = jax.random.split(jax.random.fold_in(key, 51), BATCH)
    picks = jax.vmap(lambda k: jax.random.permutation(k, LEN - 1)[:7])(row_keys).astype(jnp.int32) + 1
    starts = jnp.any(picks[:, :, None] == index_all[:, None, :], axis=1)
    starts = jnp.where(row_index == BATCH - 1, index_all == 0, starts | (index_all == 0))
    segment = jnp.cumsum(starts.astype(jnp.int32), axis=1) - 1
    row_begin = lax.cummax(jnp.where(starts, index_all, 0), axis=1)
    return (segment.astype(jnp.int32), (index_all - row_begin).astype(jnp.int32))


def draw_segment_ids(key, part):
    return document_layout(key)[0]


def draw_positions(key, part):
    return document_layout(key)[1]


def with_spikes(values, key, source, target, shards_of, factor):
    owner, partner = [(jnp.arange(values.shape[dim]) // (values.shape[dim] // shards_of)).reshape([-1 if axis == dim else 1 for axis in range(values.ndim)]) for dim in (source, target)]
    chosen = jax.random.permutation(key, shards_of)[partner]
    strong = (owner == chosen) | (owner == (partner + shards_of // 2) % shards_of)
    return jnp.where(strong, factor * values, values)


def shard_levels(own_key, extent, shards, smallest, high):
    def one(axis_at, shards_of):
        heights = jax.random.uniform(jax.random.fold_in(jax.random.fold_in(own_key, 6), axis_at), (shards_of,), jnp.float32, smallest / len(shards), high / len(shards))
        return jnp.repeat(jnp.exp(heights), extent[axis_at] // shards_of).reshape((-1,) + (1,) * (len(extent) - axis_at - 1))

    loudness = one(*shards[0])
    for cut in shards[1:]:
        loudness = loudness * one(*cut)
    return loudness


def bell_draw(stream_key, shape, scale, bound, pieces=(), kind=jnp.bfloat16):
    array = scale * jax.random.normal(stream_key, shape, jnp.float32)
    if pieces:
        array = array * shard_levels(stream_key, shape, pieces, -0.22, 0.18)
    return jnp.clip(array, -bound, bound).astype(kind)


def gaussian_with(rng, dims, deviation, reach, cuts, heavy, kind=jnp.bfloat16):
    values = deviation * jax.random.normal(rng, dims, jnp.float32)
    if cuts:
        values = values * shard_levels(rng, dims, cuts, -0.22, 0.18)
    return jnp.clip(with_spikes(values, jax.random.fold_in(rng, 3), *heavy), -reach, reach).astype(kind)


def setup_inputs(seed: int = 0) -> dict:
    seeds = jax.random.split(jax.random.key(seed), 14)
    hidden_in = draw_hidden_in(jax.random.fold_in(seeds[13], 71), 0)
    out_grad = gaussian_with(seeds[1], (LEN, BATCH, D), 1.0, 6.0, ((0, 4), (1, 4), (2, 2)), (0, 2, 4, 2.0))
    segment_ids = draw_segment_ids(jax.random.fold_in(seeds[13], 71), 0)
    positions = draw_positions(jax.random.fold_in(seeds[13], 71), 0)
    ln_gain = jnp.clip(1.0 + 0.18 * jax.random.normal(seeds[4], (D,), jnp.float32), 0.099609375, 1.8984375).astype(jnp.bfloat16)
    ln_bias = bell_draw(seeds[5], (D,), 0.5, 3.0)
    w_qkv = draw_w_qkv(jax.random.fold_in(seeds[13], 71), 0)
    qkv_bias = bell_draw(seeds[7], (3, D), 0.5, 3.0, ((1, 2),))
    w_out = bell_draw(seeds[8], (D, D), (D // 16) ** -0.5, 0.5, ((0, 16), (1, 2)))
    w_up = bell_draw(seeds[9], (D, FF), D ** -0.5, 0.125, ((0, 16), (1, 2)))
    up_bias = bell_draw(seeds[10], (FF,), 0.5, 3.0, ((0, 2),))
    w_down = bell_draw(seeds[11], (D, FF), FF ** -0.5, 0.0625, ((0, 16), (1, 2)))
    out_bias = bell_draw(seeds[12], (D,), 0.5, 3.0, ((0, 2),))
    return {"hidden_in": hidden_in, "out_grad": out_grad, "segment_ids": segment_ids, "positions": positions, "ln_gain": ln_gain, "ln_bias": ln_bias, "w_qkv": w_qkv, "qkv_bias": qkv_bias, "w_out": w_out, "w_up": w_up, "up_bias": up_bias, "w_down": w_down, "out_bias": out_bias}


@jax.custom_vjp
def low(v):
    return lax.optimization_barrier(v.astype(jnp.bfloat16)).astype(jnp.float32)

@jax.custom_vjp
def low_back(v):
    return v

def low_keep(v):
    return (low(v), None)

def low_pass(kept, grad):
    return (grad,)

def back_keep(v):
    return (v, None)

def back_low(kept, grad):
    return (low(grad),)
low.defvjp(low_keep, low_pass)
low_back.defvjp(back_keep, back_low)
eps_norm = 1e-05
highest = lax.Precision.HIGHEST

def gelu_tanh(inputs):
    inner = 0.7978845608028654 * (inputs + 0.044715 * inputs * inputs * inputs)
    return 0.5 * inputs * (1.0 + jnp.tanh(inner))

def rotary_tables(pos_flat):
    half_rot = ROT // 2
    freqs = jnp.exp(jnp.arange(half_rot, dtype=jnp.float32) * (-2.0 * math.log(10000.0) / ROT))
    angles = pos_flat.astype(jnp.float32)[:, None] * freqs[None, :]
    return (jnp.cos(angles)[:, None, :], jnp.sin(angles)[:, None, :])

def rotate_fwd(tensor, cos_tab, sin_tab):
    half_rot = ROT // 2
    first_half = tensor[..., :half_rot]
    second_half = tensor[..., half_rot:ROT]
    return jnp.concatenate([first_half * cos_tab - second_half * sin_tab, second_half * cos_tab + first_half * sin_tab, tensor[..., ROT:]], -1)

def matmul(left, right):
    return jnp.dot(left, right, preferred_element_type=jnp.float32, precision=highest)

def one_row(params, x_row, seg_row, pos_row):
    ln_gain, ln_bias, w_qkv, qkv_bias, w_out, w_up, up_bias, w_down, out_bias = params
    row_mean = lax.optimization_barrier(jnp.mean(x_row, -1, keepdims=True))
    centred = x_row - row_mean
    x_hat = centred * lax.rsqrt(lax.optimization_barrier(jnp.mean(centred * centred, -1, keepdims=True)) + eps_norm)
    normed = low(x_hat * ln_gain + ln_bias)
    q_pre = low_back(matmul(normed, w_qkv[:, 0, :]) + qkv_bias[0])
    k_pre = low_back(matmul(normed, w_qkv[:, 1, :]) + qkv_bias[1])
    v_pre = low_back(matmul(normed, w_qkv[:, 2, :]) + qkv_bias[2])
    cos_tab, sin_tab = rotary_tables(pos_row)
    queries = low(rotate_fwd(q_pre.reshape(LEN, HEADS, HD), cos_tab, sin_tab))
    keys_rot = low(rotate_fwd(k_pre.reshape(LEN, HEADS, HD), cos_tab, sin_tab))
    values = low(v_pre).reshape(LEN, HEADS, HD)
    query_block = min(512, LEN)
    n_blocks = LEN // query_block
    key_index = jnp.arange(LEN, dtype=jnp.int32)
    score_scale = 1.0 / math.sqrt(HD)

    def attend(item):
        q_block, q_seg, q_index = item
        scores = jnp.einsum('qhd,khd->hqk', q_block, keys_rot, precision=highest) * score_scale
        scores = low_back(scores)
        allowed = (q_seg[:, None] == seg_row[None, :]) & (q_index[:, None] >= key_index[None, :])
        scores = jnp.where(allowed[None], scores, -jnp.inf)
        top_score = lax.optimization_barrier(jnp.max(scores, -1, keepdims=True))
        expd = jnp.exp(scores - top_score)
        probs = expd / lax.optimization_barrier(jnp.sum(expd, -1, keepdims=True))
        prob_low = low(probs)
        return jnp.einsum('hqk,khd->qhd', prob_low, values, precision=highest)
    attended = lax.map(jax.checkpoint(attend), (queries.reshape(n_blocks, query_block, HEADS, HD), seg_row.reshape(n_blocks, query_block), key_index.reshape(n_blocks, query_block)))
    attn_in = low(low_back(attended.reshape(LEN, D)))
    up_lin = low_back(matmul(normed, w_up) + up_bias)
    act_out = low(gelu_tanh(up_lin))
    return x_row + matmul(attn_in, w_out.T) + matmul(act_out, w_down.T) + out_bias

def reference(hidden_in, out_grad, segment_ids, positions, ln_gain, ln_bias, w_qkv, qkv_bias, w_out, w_up, up_bias, w_down, out_bias):
    params = tuple((p.astype(jnp.float32) for p in (ln_gain, ln_bias, w_qkv, qkv_bias, w_out, w_up, up_bias, w_down, out_bias)))
    x_rows = jnp.transpose(hidden_in.astype(jnp.float32), (1, 0, 2))

    def forward(weights, inputs):

        def step(carry, item):
            x_row, seg_row, pos_row = item
            return (carry, one_row(weights, x_row, seg_row, pos_row))
        _, outputs = lax.scan(step, jnp.zeros((), jnp.float32), (inputs, segment_ids, positions))
        return outputs
    outputs, pull = jax.vjp(forward, params, x_rows)
    grads_params, grads_x = pull(jnp.transpose(out_grad.astype(jnp.float32), (1, 0, 2)))
    gain_grad, lnb_grad, qkv_grad, bias_grad, wout_grad, wup_grad, upb_grad, wdown_grad, outb_grad = grads_params
    block_out = jnp.transpose(outputs, (1, 0, 2)).astype(jnp.bfloat16)
    input_grad = jnp.transpose(grads_x, (1, 0, 2))
    return (block_out, input_grad, gain_grad, lnb_grad, qkv_grad, bias_grad, wout_grad, wup_grad, upb_grad, wdown_grad, outb_grad)
```

```python
import math

import jax
import jax.numpy as jnp
from jax import lax
from jax.sharding import PartitionSpec as P

HD = 64
ROT = 32
EPS = 1e-05
F32 = jnp.float32
BF16 = jnp.bfloat16
DIRECT = 4


def gelu_tanh(inputs):
    inner = 0.7978845608028654 * (inputs + 0.044715 * inputs * inputs * inputs)
    return 0.5 * inputs * (1.0 + jnp.tanh(inner))


def rotary_tables(pos_flat):
    half_rot = ROT // 2
    freqs = jnp.exp(jnp.arange(half_rot, dtype=F32) * (-2.0 * math.log(10000.0) / ROT))
    angles = pos_flat.astype(F32)[:, None] * freqs[None, :]
    return (jnp.cos(angles)[:, None, :], jnp.sin(angles)[:, None, :])


def rotate(tensor, cos_tab, sin_tab):
    half_rot = ROT // 2
    first = tensor[..., :half_rot]
    second = tensor[..., half_rot:ROT]
    return jnp.concatenate(
        [first * cos_tab - second * sin_tab, second * cos_tab + first * sin_tab, tensor[..., ROT:]],
        -1,
    )


def swap(value, axis, bit):
    n = lax.axis_size(axis)
    return lax.ppermute(value, axis, [(i, i ^ bit) for i in range(n)])


def bits_of(n):
    return [1 << b for b in range(n.bit_length() - 1)]


def sum_over(value, axis):
    for bit in bits_of(lax.axis_size(axis)):
        value = value + swap(value, axis, bit)
    return value


def stack_over(value, axis):
    n = lax.axis_size(axis)
    if n > DIRECT:
        return lax.all_gather(value, axis)
    at = lax.axis_index(axis)
    out = jnp.zeros((n,) + value.shape, value.dtype)
    out = lax.dynamic_update_index_in_dim(out, value, at, 0)
    for s in range(1, n):
        came = lax.ppermute(value, axis, [(i, (i + s) % n) for i in range(n)])
        out = lax.dynamic_update_index_in_dim(out, came, (at - s) % n, 0)
    return out


def deal(chunks, axis):
    n = chunks.shape[0]
    if n > DIRECT:
        return lax.all_to_all(chunks, axis, 0, 0)
    at = lax.axis_index(axis)
    out = chunks
    for s in range(1, n):
        sent = lax.dynamic_index_in_dim(chunks, (at + s) % n, 0, keepdims=False)
        came = lax.ppermute(sent, axis, [(i, (i + s) % n) for i in range(n)])
        out = lax.dynamic_update_index_in_dim(out, came, (at - s) % n, 0)
    return out


def gather_tokens(block):
    n_c, n_t = lax.axis_size("ctx"), lax.axis_size("tp")
    tokens, half = block.shape
    if n_c > DIRECT or n_t != 2:
        wide = lax.all_gather(block, "tp", axis=1, tiled=True)
        return lax.all_gather(wide, "ctx", axis=0, tiled=True)
    c_at, t_at = lax.axis_index("ctx"), lax.axis_index("tp")

    def across(value, who):
        return lax.ppermute(
            value, ("ctx", "tp"), [(c * 2 + t, c * 2 + 1 - t) for c in who for t in range(2)]
        )

    right = {0: block}
    left = {0: block}
    far = {0: across(block, range(n_c))}
    far_right, far_left = {}, {}
    for s in range(1, n_c):
        right[s] = lax.ppermute(right[s - 1], "ctx", [(i, i + 1) for i in range(s - 1, n_c - 1)])
        left[s] = lax.ppermute(left[s - 1], "ctx", [(i, i - 1) for i in range(1, n_c - s + 1)])
        far_right[s] = across(right[s], range(s, n_c))
        far_left[s] = across(left[s], range(0, n_c - s))
    out = jnp.zeros((n_c * tokens, 2 * half), block.dtype)

    def put(out, near, other, slot):
        out = lax.dynamic_update_slice(out, near, (slot * tokens, t_at * half))
        return lax.dynamic_update_slice(out, other, (slot * tokens, (1 - t_at) * half))

    out = put(out, block, far[0], c_at)
    for s in range(1, n_c):
        near = jnp.where(c_at >= s, right[s], left[n_c - s])
        other = jnp.where(c_at >= s, far_right[s], far_left[n_c - s])
        out = put(out, near, other, (c_at - s) % n_c)
    return out


def gather_rows(block):
    n_f = lax.axis_size("fsdp")
    f_at = lax.axis_index("fsdp")
    held = {0: block}
    for bit in reversed(bits_of(n_f)):
        for k in list(held):
            held[k | bit] = swap(held[k], "fsdp", bit)
    rows = block.shape[0]
    out = jnp.zeros((n_f * rows, block.shape[1]), block.dtype)
    for k, piece in held.items():
        out = lax.dynamic_update_slice(out, piece, ((f_at ^ k) * rows, 0))
    return out


def reduce_rows(make):
    n_f = lax.axis_size("fsdp")
    held = None
    span = list(range(n_f))
    for bit in bits_of(n_f):
        keep = [k for k in span if not k & bit]
        gone = [k for k in span if k & bit]
        out = {k: (make(k) if held is None else held[k]).astype(BF16) for k in gone}
        came = {k ^ bit: swap(out[k], "fsdp", bit) for k in gone}
        held = {k: (make(k) if held is None else held[k]) + came[k].astype(F32) for k in keep}
        span = keep
    return held[0]


def scatter_tokens(make, tokens):
    n_c = lax.axis_size("ctx")
    away = swap(make(1).astype(BF16), "tp", 1)
    part = make(0) + away.astype(F32)
    blocks = part.reshape(n_c, tokens, part.shape[1])
    came = deal(blocks.astype(BF16), "ctx")
    at = lax.axis_index("ctx")
    own = lax.dynamic_index_in_dim(blocks, at, 0, keepdims=False)
    mine = (jnp.arange(n_c) == at)[:, None, None]
    return own + jnp.sum(jnp.where(mine, 0.0, came.astype(F32)), 0)


def local(
    hidden_in,
    out_grad,
    segment_ids,
    positions,
    ln_gain,
    ln_bias,
    w_qkv,
    qkv_bias,
    w_out,
    w_up,
    up_bias,
    w_down,
    out_bias,
):
    l_dev, rows_b, half_d = hidden_in.shape
    n_f, n_c, n_t = (lax.axis_size(a) for a in ("fsdp", "ctx", "tp"))
    width = half_d * n_t
    length = l_dev * n_c
    own_tok = l_dev * rows_b
    tokens = length * rows_b
    att = half_d // n_c
    heads = att // HD
    ff_half = w_up.shape[1]
    ff = ff_half // n_c
    shard = w_up.shape[0]
    t_at, c_at, f_at = lax.axis_index("tp"), lax.axis_index("ctx"), lax.axis_index("fsdp")
    scale = 1.0 / math.sqrt(HD)

    own_x = hidden_in.reshape(own_tok, half_d)
    own_g = out_grad.reshape(own_tok, half_d)
    x_all = gather_tokens(own_x)

    def spread(weight, cols):
        chunks = jnp.moveaxis(weight.reshape(shard, -1, n_c, cols), 2, 0).reshape(n_c, shard, -1)
        return gather_rows(deal(chunks, "ctx").reshape(n_c * shard, -1))

    qkv_w = spread(w_qkv, att)
    up_w = spread(w_up, ff)
    g_all = gather_tokens(own_g)
    out_w = spread(w_out, att)
    down_w = spread(w_down, ff)

    def norm_of(value):
        value = value.astype(F32)
        mean = jnp.mean(value, -1, keepdims=True)
        centred = value - mean
        inv = lax.rsqrt(jnp.mean(centred * centred, -1, keepdims=True) + EPS)
        return centred * inv, mean, inv

    x_hat, row_mean, inv_std = norm_of(x_all)
    normed = (x_hat * ln_gain.astype(F32) + ln_bias.astype(F32)).astype(BF16)

    lin_qkv = jnp.dot(normed, qkv_w, preferred_element_type=F32).reshape(tokens, 3, heads, HD)
    qkv_b = lax.dynamic_slice_in_dim(qkv_bias, c_at * att, att, 1).astype(F32).reshape(3, heads, HD)
    cos_tab, sin_tab = rotary_tables(positions.T.reshape(tokens))

    def split(value):
        return value.reshape(length, rows_b, heads, HD)

    queries = split(rotate(lin_qkv[:, 0] + qkv_b[0], cos_tab, sin_tab).astype(BF16))
    keys = split(rotate(lin_qkv[:, 1] + qkv_b[1], cos_tab, sin_tab).astype(BF16))
    values = split((lin_qkv[:, 2] + qkv_b[2]).astype(BF16))
    index = jnp.arange(length, dtype=jnp.int32)
    allowed = (segment_ids[:, :, None] == segment_ids[:, None, :]) & (
        index[:, None] >= index[None, :]
    )[None]
    scores = jnp.einsum("qrhd,krhd->rhqk", queries, keys, preferred_element_type=F32) * scale
    scores = jnp.where(allowed[:, None], scores, -jnp.inf)
    best = jnp.max(scores, -1, keepdims=True)
    expd = jnp.exp(scores - best)
    probs = expd / jnp.sum(expd, -1, keepdims=True)
    prob_low = probs.astype(BF16)
    attended = jnp.einsum("rhqk,krhd->qrhd", prob_low, values, preferred_element_type=F32)
    attn_in = attended.astype(BF16).reshape(tokens, att)

    up_b = lax.dynamic_slice_in_dim(up_bias, c_at * ff, ff, 0).astype(F32)
    up_lin = jnp.dot(normed, up_w, preferred_element_type=F32) + up_b
    act_out = gelu_tanh(up_lin).astype(BF16)

    def half_of(value, u, axis):
        return lax.dynamic_slice_in_dim(value, (t_at ^ u) * half_d, half_d, axis)

    def out_term(u):
        return jnp.einsum(
            "tf,nf->tn", attn_in, half_of(out_w, u, 0), preferred_element_type=F32
        ) + jnp.einsum("tf,nf->tn", act_out, half_of(down_w, u, 0), preferred_element_type=F32)

    branch = scatter_tokens(out_term, own_tok)
    block_out = (own_x.astype(F32) + branch + out_bias.astype(F32)).astype(BF16)

    rows_f = width // n_f

    def cols_of(value, k):
        return lax.dynamic_slice_in_dim(value, (f_at ^ k) * rows_f, rows_f, 1)

    def grad_rows(left, right):
        return reduce_rows(
            lambda k: jnp.einsum(
                "tn,tc->nc", cols_of(left, k), right, preferred_element_type=F32
            )
        )

    def deliver(total, parts):
        cols = total.shape[1]
        came = deal(total.astype(BF16).reshape(n_c, shard, cols), "ctx").astype(F32)
        return jnp.moveaxis(came.reshape(n_c, shard, parts, cols // parts), 0, 2).reshape(
            shard, parts, -1
        )

    down_grad = deliver(grad_rows(g_all, act_out), 1).reshape(shard, ff_half)
    out_weight_grad = deliver(grad_rows(g_all, attn_in), 1).reshape(shard, half_d)

    d_act = jnp.dot(g_all, down_w, preferred_element_type=F32)
    _, gelu_pull = jax.vjp(gelu_tanh, up_lin)
    d_up = gelu_pull(d_act)[0].astype(BF16)
    up_grad = deliver(grad_rows(normed, d_up), 1).reshape(shard, ff_half)

    d_att = split(jnp.dot(g_all, out_w, preferred_element_type=F32).astype(BF16))
    delta = jnp.sum(d_att.astype(F32) * attended, -1)
    d_prob = jnp.einsum("qrhd,krhd->rhqk", d_att, values, preferred_element_type=F32)
    d_score = (probs * (d_prob - jnp.transpose(delta, (1, 2, 0))[..., None])).astype(BF16)
    dq = jnp.einsum("rhqk,krhd->qrhd", d_score, keys, preferred_element_type=F32) * scale
    dk = jnp.einsum("rhqk,qrhd->krhd", d_score, queries, preferred_element_type=F32) * scale
    dv = jnp.einsum("rhqk,qrhd->krhd", prob_low, d_att, preferred_element_type=F32)

    def flat(value):
        return value.reshape(tokens, heads, HD)

    d_qkv = jnp.stack(
        [
            rotate(flat(dq), cos_tab, -sin_tab).astype(BF16),
            rotate(flat(dk), cos_tab, -sin_tab).astype(BF16),
            flat(dv).astype(BF16),
        ],
        1,
    ).reshape(tokens, 3 * att)

    def norm_term(u):
        return jnp.einsum(
            "tc,nc->tn", d_qkv, half_of(qkv_w, u, 0), preferred_element_type=F32
        ) + jnp.einsum("tc,nc->tn", d_up, half_of(up_w, u, 0), preferred_element_type=F32)

    d_norm = scatter_tokens(norm_term, own_tok)
    qkv_grad = deliver(grad_rows(normed, d_qkv), 3)

    mine = lambda v: lax.dynamic_slice_in_dim(v, c_at * own_tok, own_tok, 0)
    own_inv = mine(inv_std)
    own_hat = (own_x.astype(F32) - mine(row_mean)) * own_inv
    d_hat = d_norm * lax.dynamic_slice_in_dim(ln_gain, t_at * half_d, half_d, 0).astype(F32)
    sums = jnp.stack([jnp.sum(d_hat, -1), jnp.sum(d_hat * own_hat, -1)])
    sums = sum_over(sums, "tp") / width
    d_ln = own_inv * (d_hat - sums[0][:, None] - own_hat * sums[1][:, None])
    input_grad = d_ln + own_g.astype(F32)

    early = jnp.concatenate(
        [
            jnp.sum(half_of(g_all, 0, 1).astype(F32), 0),
            jnp.sum(d_up.astype(F32), 0),
            jnp.sum(d_qkv.astype(F32), 0),
        ]
    )
    early = sum_over(early, "fsdp")
    outb_grad = early[:half_d]
    rest = stack_over(early[half_d:], "ctx")
    upb_grad = rest[:, :ff].reshape(ff_half)
    bias_grad = jnp.moveaxis(rest[:, ff:].reshape(n_c, 3, att), 0, 1).reshape(3, half_d)
    late = jnp.stack([jnp.sum(d_norm * own_hat, 0), jnp.sum(d_norm, 0)])
    late = sum_over(sum_over(late, "ctx"), "fsdp")
    return (
        block_out.reshape(l_dev, rows_b, half_d),
        input_grad.reshape(l_dev, rows_b, half_d),
        late[0],
        late[1],
        qkv_grad,
        bias_grad,
        out_weight_grad,
        up_grad,
        upb_grad,
        down_grad,
        outb_grad,
    )


def solution(mesh):
    return jax.shard_map(
        local,
        mesh=mesh,
        in_specs=(
            P("ctx", "fsdp", "tp"),
            P("ctx", "fsdp", "tp"),
            P("fsdp", None),
            P("fsdp", None),
            P(),
            P(),
            P(("fsdp", "ctx"), None, "tp"),
            P(None, "tp"),
            P(("fsdp", "ctx"), "tp"),
            P(("fsdp", "ctx"), "tp"),
            P("tp"),
            P(("fsdp", "ctx"), "tp"),
            P("tp"),
        ),
        out_specs=(
            P("ctx", "fsdp", "tp"),
            P("ctx", "fsdp", "tp"),
            P("tp"),
            P("tp"),
            P(("fsdp", "ctx"), None, "tp"),
            P(None, "tp"),
            P(("fsdp", "ctx"), "tp"),
            P(("fsdp", "ctx"), "tp"),
            P("tp"),
            P(("fsdp", "ctx"), "tp"),
            P("tp"),
        ),
        check_vma=False,
    )
```

```python
import functools
import math

import jax
import jax.numpy as jnp
from jax import lax
from jax.experimental import pallas as pl
from jax.experimental.pallas import tpu as pltpu
from jax.sharding import PartitionSpec as P

HD = 64
ROT = 32
EPS = 1e-05
NEVER = -1e30
BLOCK = 256
F32 = jnp.float32
BF16 = jnp.bfloat16


def run(kernel, where, grid, ins, in_specs, outs, out_specs, scratch=(), flops=0):
    moved = sum(math.prod(v.shape) * v.dtype.itemsize for v in (*ins, *outs))
    return pl.pallas_call(
        kernel,
        grid_spec=pltpu.PrefetchScalarGridSpec(
            num_scalar_prefetch=1,
            grid=grid,
            in_specs=in_specs,
            out_specs=out_specs,
            scratch_shapes=scratch,
        ),
        out_shape=outs,
        compiler_params=pltpu.CompilerParams(
            dimension_semantics=("arbitrary",) * len(grid), vmem_limit_bytes=56 << 20
        ),
        cost_estimate=pl.CostEstimate(flops=flops, bytes_accessed=moved, transcendentals=0),
    )(where, *ins)


def shape(dims, kind=BF16):
    return jax.ShapeDtypeStruct(dims, kind)


def whole_spec(value):
    return pl.BlockSpec(value.shape, lambda *_: (0,) * value.ndim)


def rows_spec(cols, block=BLOCK):
    return pl.BlockSpec((block, cols), lambda i, *_: (i, 0))


def dot(left, right, dims=((1,), (0,))):
    return lax.dot_general(left, right, (dims, ((), ())), preferred_element_type=F32)


def turn(value, cos_t, low_t, high_t, half):
    n = value.shape[-1]
    reps = n // cos_t.shape[-1]
    if reps > 1:
        cos_t, low_t, high_t = (jnp.concatenate([v] * reps, -1) for v in (cos_t, low_t, high_t))
    up = pltpu.roll(value, n - half, value.ndim - 1)
    down = pltpu.roll(value, half, value.ndim - 1)
    return value * cos_t + up * low_t + down * high_t


def k_qkv(at, mine, other, gain, bias, w0, w1, w2, w3, qb, cos_t, low_t, high_t, normed, q, k, v):
    f_at, t_at = at[0], at[2]
    half = mine.shape[1]
    width = 2 * half
    a, b = mine[...].astype(F32), other[...].astype(F32)
    mean = (jnp.sum(a, -1, keepdims=True) + jnp.sum(b, -1, keepdims=True)) / width
    a, b = a - mean, b - mean
    var = (jnp.sum(a * a, -1, keepdims=True) + jnp.sum(b * b, -1, keepdims=True)) / width
    inv = lax.rsqrt(var + EPS)
    for part, slot in ((a, t_at), (b, 1 - t_at)):
        line = part * inv * gain[slot].astype(F32) + bias[slot].astype(F32)
        normed[:, pl.ds(pl.multiple_of(slot * half, half), half)] = line.astype(BF16)
    acc = qb[...]
    for n, w in enumerate((w0, w1, w2, w3)):
        rows = w.shape[0]
        at_col = pl.multiple_of((f_at ^ n) * rows, rows)
        acc = acc + dot(normed[:, pl.ds(at_col, rows)], w[...])
    att = q.shape[1]
    tables = (cos_t[...], low_t[...], high_t[...])
    q[...] = turn(acc[:, :att], *tables, ROT // 2).astype(BF16)
    k[...] = turn(acc[:, att : 2 * att], *tables, ROT // 2).astype(BF16)
    v[...] = acc[:, 2 * att :].astype(BF16)


def k_up(at, normed, w0, w1, w2, w3, ub, act, slope):
    f_at = at[0]
    acc = ub[...]
    for n, w in enumerate((w0, w1, w2, w3)):
        rows = w.shape[0]
        at_col = pl.multiple_of((f_at ^ n) * rows, rows)
        acc = acc + dot(normed[:, pl.ds(at_col, rows)], w[...])
    c0, c1 = 0.7978845608028654, 0.044715
    square = acc * acc
    bent = jnp.tanh(c0 * acc * (1.0 + c1 * square))
    act[...] = (0.5 * acc * (1.0 + bent)).astype(BF16)
    slope[...] = (
        0.5 * (1.0 + bent) + 0.5 * acc * (1.0 - bent * bent) * c0 * (1.0 + 3.0 * c1 * square)
    ).astype(BF16)


def head_masks(width):
    lane = lax.broadcasted_iota(jnp.int32, (1, width), 1)
    return [lane // HD == h for h in range(width // HD)]


def pair_mask(seg_col, seg_row, start, rows, keys):
    row = start + lax.broadcasted_iota(jnp.int32, (rows, keys), 0)
    col = lax.broadcasted_iota(jnp.int32, (rows, keys), 1)
    same = seg_col[0, pl.ds(start, rows), :] == seg_row[0, :, pl.ds(0, keys)]
    return jnp.where(same & (row >= col), 0.0, NEVER)


def k_attend(at, q, k, v, seg_col, seg_row, out, lse):
    length, width = q.shape[1:]
    rows = min(256, length)
    heads = head_masks(width)
    for i in range(length // rows):
        span, keys = pl.ds(i * rows, rows), (i + 1) * rows
        mask = pair_mask(seg_col, seg_row, i * rows, rows, keys)
        q_i, k_i, v_i = q[0, span, :], k[0, pl.ds(0, keys), :], v[0, pl.ds(0, keys), :]
        total = jnp.zeros((rows, width), F32)
        logs = jnp.zeros((rows, width), F32)
        for mine in heads:
            q_h = jnp.where(mine, q_i, 0) * jnp.asarray(1.0 / math.sqrt(HD), BF16)
            scores = dot(q_h, k_i, ((1,), (1,))) + mask
            top = jnp.max(scores, -1, keepdims=True)
            weights = jnp.exp(scores - top)
            mass = jnp.sum(weights, -1, keepdims=True)
            got = dot(weights.astype(BF16), v_i) / mass
            total = jnp.where(mine, got, total)
            logs = jnp.where(mine, top + jnp.log(mass), logs)
        out[0, span, :] = total.astype(BF16)
        lse[0, span, :] = logs


def k_attend_back(
    at, q, k, v, d_out, lse, seg_col, seg_row, cos_t, low_t, high_t, dq, dk, dv, sums, k_acc, v_acc
):
    length, width = q.shape[1:]
    rows = min(256, length)
    heads = head_masks(width)
    scale = jnp.asarray(1.0 / math.sqrt(HD), BF16)
    k_acc[...] = jnp.zeros_like(k_acc)
    v_acc[...] = jnp.zeros_like(v_acc)
    q_sum = jnp.zeros((1, width), F32)
    for i in range(length // rows):
        span, keys = pl.ds(i * rows, rows), (i + 1) * rows
        mask = pair_mask(seg_col, seg_row, i * rows, rows, keys)
        q_i, d_i = q[0, span, :], d_out[0, span, :]
        k_i, v_i = k[0, pl.ds(0, keys), :], v[0, pl.ds(0, keys), :]
        dq_i = jnp.zeros((rows, width), F32)
        dk_i = jnp.zeros((keys, width), F32)
        dv_i = jnp.zeros((keys, width), F32)
        for h, mine in enumerate(heads):
            q_h = jnp.where(mine, q_i, 0) * scale
            d_h = jnp.where(mine, d_i, 0)
            k_h = jnp.where(mine, k_i, 0) * scale
            scores = dot(q_h, k_i, ((1,), (1,))) + mask
            probs = jnp.exp(scores - lse[0, span, h * HD : h * HD + 1])
            d_prob = dot(d_h, v_i, ((1,), (1,)))
            delta = jnp.sum(probs * d_prob, -1, keepdims=True)
            d_score = (probs * (d_prob - delta)).astype(BF16)
            dq_i = dq_i + dot(d_score, k_h)
            dk_i = dk_i + dot(d_score, q_h, ((0,), (0,)))
            dv_i = dv_i + dot(probs.astype(BF16), d_h, ((0,), (0,)))
        k_acc[pl.ds(0, keys), :] += dk_i
        v_acc[pl.ds(0, keys), :] += dv_i
        tables = (cos_t[0, span, :], -low_t[0, span, :], -high_t[0, span, :])
        line = turn(dq_i, *tables, ROT // 2).astype(BF16)
        dq[0, span, :] = line
        q_sum = q_sum + jnp.sum(line.astype(F32), 0, keepdims=True)
    tables = (cos_t[0], -low_t[0], -high_t[0])
    line_k = turn(k_acc[...], *tables, ROT // 2).astype(BF16)
    line_v = v_acc[...].astype(BF16)
    dk[0] = line_k
    dv[0] = line_v
    sums[0, 0:1, :] = q_sum
    sums[0, 1:2, :] = jnp.sum(line_k.astype(F32), 0, keepdims=True)
    sums[0, 2:3, :] = jnp.sum(line_v.astype(F32), 0, keepdims=True)


def put_half(value, n, at, keep, away, halves):
    f_at, t_at = at[0], at[2]
    block = f_at ^ n
    cols = value.shape[1]
    here = pl.ds(pl.multiple_of((block % halves) * cols, cols), cols)
    own = block // halves == t_at

    @pl.when(own)
    def _():
        keep[:, here] = value.astype(keep.dtype)

    @pl.when(jnp.logical_not(own))
    def _():
        away[:, here] = value.astype(away.dtype)


def k_out(at, attn, act, w0, w1, w2, w3, out):
    f_at = at[0]
    att = attn.shape[1]
    for n, w in enumerate((w0, w1, w2, w3)):
        term = dot(attn[...], w[:, :att], ((1,), (1,))) + dot(act[...], w[:, att:], ((1,), (1,)))
        block = f_at ^ n
        cols = w.shape[0]
        out[0, block // 2, :, pl.ds(pl.multiple_of((block % 2) * cols, cols), cols)] = term.astype(
            BF16
        )


def k_norm_back(at, dq, dk, dv, d_up, a0, a1, a2, a3, w0, w1, w2, w3, keep, away):
    att = dq.shape[1]
    for n, (a, w) in enumerate(((a0, w0), (a1, w1), (a2, w2), (a3, w3))):
        term = dot(d_up[...], w[...], ((1,), (1,)))
        for p, d in enumerate((dq, dk, dv)):
            term = term + dot(d[...], a[:, p * att : (p + 1) * att], ((1,), (1,)))
        put_half(term, n, at, keep, away, 2)


def k_out_back(at, g, slope, w0, w1, w2, w3, d_att, d_up, sums):
    f_at = at[0]
    att = d_att.shape[1]
    acc = None
    for n, w in enumerate((w0, w1, w2, w3)):
        block = f_at ^ n
        rows = w.shape[0]
        cols = pl.ds(pl.multiple_of((block % 2) * rows, rows), rows)
        term = dot(g[0, block // 2, :, cols], w[...])
        acc = term if acc is None else acc + term
    d_att[...] = acc[:, :att].astype(BF16)
    line = (acc[:, att:] * slope[...].astype(F32)).astype(BF16)
    d_up[...] = line

    @pl.when(pl.program_id(0) == 0)
    def _():
        sums[...] = jnp.zeros_like(sums)

    sums[...] += jnp.sum(line.astype(F32), 0, keepdims=True)


def k_grad(at, left, *rest, adds):
    rights, out = rest[: -1 - adds], rest[-1]
    lhs = left[...]
    lhs = lhs.reshape(-1, lhs.shape[-1])
    col = 0
    for right in rights:
        n = right.shape[1]
        term = dot(lhs, right[...], ((0,), (0,)))
        if adds:
            term = term + rest[-2][0, :, col : col + n].astype(F32)
        out[0, :, col : col + n] = term.astype(out.dtype)
        col += n


def swap(value, axis, bit):
    n = lax.axis_size(axis)
    return lax.ppermute(value, axis, [(i, i ^ bit) for i in range(n)])


def dealt(chunks, axis):
    return lax.all_to_all(chunks, axis, 0, 0)


def shown(value, axis):
    axes = (axis,) if isinstance(axis, str) else axis
    n = math.prod(lax.axis_size(a) for a in axes)
    return dealt(jnp.broadcast_to(value[None], (n,) + value.shape), axis)


def after(value, *earlier):
    return lax.optimization_barrier((value, *earlier))[0]


def rotary_tables(pos, lanes):
    lane = jnp.arange(lanes, dtype=jnp.int32) % HD
    half = ROT // 2
    freqs = jnp.exp((lane % half).astype(F32) * (-2.0 * math.log(10000.0) / ROT))
    freqs = jnp.where(lane < ROT, freqs, 0.0)
    angles = pos.astype(F32)[:, None] * freqs[None, :]
    sines = jnp.sin(angles)
    return (
        jnp.cos(angles),
        jnp.where(lane < half, -sines, 0.0),
        jnp.where((lane >= half) & (lane < ROT), sines, 0.0),
    )


def local(
    hidden_in,
    out_grad,
    segment_ids,
    positions,
    ln_gain,
    ln_bias,
    w_qkv,
    qkv_bias,
    w_out,
    w_up,
    up_bias,
    w_down,
    out_bias,
):
    l_dev, rows_b, half_d = hidden_in.shape
    n_f, n_c, n_t = (lax.axis_size(a) for a in ("fsdp", "ctx", "tp"))
    assert n_f == 4 and n_t == 2
    width = half_d * n_t
    length = l_dev * n_c
    own_tok = l_dev * rows_b
    tokens = length * rows_b
    att = half_d // n_c
    ff_half = w_up.shape[1]
    ff = ff_half // n_c
    shard = w_up.shape[0]
    lanes = min(2 * HD, att)
    groups = att // lanes
    t_at, c_at, f_at = lax.axis_index("tp"), lax.axis_index("ctx"), lax.axis_index("fsdp")
    where = jnp.stack([f_at, c_at, t_at]).astype(jnp.int32)
    steps = (n_c,)
    piece = n_c * shard

    own_x = hidden_in.reshape(own_tok, half_d)
    own_g = out_grad.reshape(own_tok, half_d)

    def chunks_of(weight, cols):
        parts = weight.reshape(shard, -1, n_c, cols)
        return jnp.moveaxis(parts, 2, 0).reshape(n_c, shard, -1)

    def spread(chunks):
        mine = dealt(chunks, "ctx").reshape(piece, -1)
        across = swap(mine, "fsdp", 2)
        return mine, (mine, swap(mine, "fsdp", 1), across, swap(across, "fsdp", 1))

    x_mine = shown(own_x, "ctx").reshape(tokens, half_d)
    x_other = swap(x_mine, "tp", 1)
    first, qkv_w = spread(after(chunks_of(w_qkv, att), x_mine))
    g_all = lax.all_gather(after(own_g, x_mine), ("ctx", "tp"), axis=0).reshape(
        n_c, n_t, own_tok, half_d
    )
    second, up_w = spread(after(chunks_of(w_up, ff), first))
    outdown = jnp.concatenate([chunks_of(w_out, att), chunks_of(w_down, ff)], 2)
    third, od_w = spread(after(outdown, second))

    tables = rotary_tables(positions.T.reshape(tokens), lanes)
    qkv_b = lax.dynamic_slice_in_dim(qkv_bias, c_at * att, att, 1).astype(F32).reshape(1, -1)
    up_b = lax.dynamic_slice_in_dim(up_bias, c_at * ff, ff, 0).astype(F32).reshape(1, -1)
    gain2 = ln_gain.reshape(n_t, 1, half_d)
    bias2 = ln_bias.reshape(n_t, 1, half_d)

    def fixed(*values):
        return [whole_spec(v) for v in values]

    def each(*cols):
        return [rows_spec(c, own_tok) for c in cols]

    normed, q, k, v = run(
        k_qkv,
        where,
        steps,
        (x_mine, x_other, gain2, bias2, *qkv_w, qkv_b, *tables),
        each(half_d, half_d) + fixed(gain2, bias2, *qkv_w, qkv_b) + each(lanes, lanes, lanes),
        [shape((tokens, width))] + [shape((tokens, att))] * 3,
        each(width, att, att, att),
        flops=2 * tokens * width * 3 * att,
    )

    def by_row(value):
        return jnp.moveaxis(value.reshape(length, rows_b, -1), 1, 0)

    def by_token(value):
        return jnp.moveaxis(value, 0, 1).reshape(tokens, -1)

    group = pl.BlockSpec((1, length, lanes), lambda r, h, *_: (r, 0, h))
    table = pl.BlockSpec((1, length, lanes), lambda r, h, *_: (r, 0, 0))
    seg_specs = [
        pl.BlockSpec((1, length, 1), lambda r, h, *_: (r, 0, 0)),
        pl.BlockSpec((1, 1, length), lambda r, h, *_: (r, 0, 0)),
    ]
    segs = (segment_ids[:, :, None], segment_ids[:, None, :])
    row_shape = (rows_b, length, att)
    pairs = rows_b * length * length * att
    q_r, k_r, v_r = by_row(q), by_row(k), by_row(v)
    attn_r, lse = run(
        k_attend,
        where,
        (rows_b, groups),
        (q_r, k_r, v_r, *segs),
        [group] * 3 + seg_specs,
        [shape(row_shape), shape(row_shape, F32)],
        [group] * 2,
        flops=4 * pairs,
    )
    attn = by_token(attn_r)

    act, slope = run(
        k_up,
        where,
        steps,
        (normed, *up_w, up_b),
        each(width) + fixed(*up_w, up_b),
        [shape((tokens, ff))] * 2,
        each(ff, ff),
        flops=2 * tokens * width * ff,
    )
    both = pl.BlockSpec((1, n_t, own_tok, half_d), lambda i, *_: (i, 0, 0, 0))
    (out_part,) = run(
        k_out,
        where,
        steps,
        (attn, act, *od_w),
        each(att, ff) + fixed(*od_w),
        [shape((n_c, n_t, own_tok, half_d))],
        [both],
        flops=2 * tokens * width * (att + ff),
    )
    branch = lax.psum_scatter(
        out_part.reshape(n_c * n_t, own_tok, half_d), ("ctx", "tp"), scatter_dimension=0
    )
    block_out = (own_x.astype(F32) + branch.astype(F32) + out_bias.astype(F32)).astype(BF16)

    def grad_rows(left, left_spec, rights):
        cols = sum(v.shape[1] for v in rights)
        dims = (2, piece, cols)
        result = pl.BlockSpec((1, piece, cols), lambda i, *_: (i, 0, 0))
        flops = tokens * width * cols

        def half(parity, *came):
            return run(
                functools.partial(k_grad, adds=len(came)),
                where,
                (2,),
                (left, *rights, *came),
                [left_spec(parity)] + fixed(*rights) + [result] * len(came),
                [shape(dims)],
                [result],
                flops=flops,
            )[0]

        came = swap(half(1), "fsdp", 1)
        kept = half(0, came)
        x_at = f_at // 2
        came = swap(lax.dynamic_index_in_dim(kept, 1 - x_at, 0, keepdims=False), "fsdp", 2)
        own = lax.dynamic_index_in_dim(kept, x_at, 0, keepdims=False)
        total = (own.astype(F32) + came.astype(F32)).astype(BF16)
        return dealt(total.reshape(n_c, shard, cols), "ctx").astype(F32)

    def laid(value, parts):
        parted = value.reshape(n_c, shard, parts, -1)
        return jnp.moveaxis(parted, 0, 2).reshape(shard, parts, -1)

    def g_spec(parity):
        return pl.BlockSpec(
            (n_c, 1, own_tok, piece), lambda i, at: (0, i, 0, (at[0] + parity) % 2)
        )

    def n_spec(parity):
        return pl.BlockSpec((tokens, piece), lambda i, at: (0, 2 * i + (at[0] + parity) % 2))

    came = grad_rows(g_all, g_spec, (attn, act))
    out_weight_grad = laid(came[..., :att], 1).reshape(shard, half_d)
    down_grad = laid(came[..., att:], 1).reshape(shard, ff_half)

    d_att, d_up, up_sum = run(
        k_out_back,
        where,
        steps,
        (g_all, slope, *od_w),
        [both] + each(ff) + fixed(*od_w),
        [shape((tokens, att)), shape((tokens, ff)), shape((1, ff), F32)],
        each(att, ff) + [pl.BlockSpec((1, ff), lambda i, *_: (0, 0))],
        flops=2 * tokens * width * (att + ff),
    )
    came = grad_rows(normed, n_spec, (d_up,))
    up_grad = laid(came, 1).reshape(shard, ff_half)

    row_tables = [by_row(v) for v in tables]
    dq, dk, dv, qkv_sums = run(
        k_attend_back,
        where,
        (rows_b, groups),
        (q_r, k_r, v_r, by_row(d_att), lse, *segs, *row_tables),
        [group] * 5 + seg_specs + [table] * 3,
        [shape(row_shape)] * 3 + [shape((rows_b * groups, 8, lanes), F32)],
        [group] * 3
        + [pl.BlockSpec((1, 8, lanes), lambda r, h, *_: (r * groups + h, 0, 0))],
        [pltpu.VMEM((length, lanes), F32)] * 2,
        flops=10 * pairs,
    )
    d_qkv = tuple(by_token(d) for d in (dq, dk, dv))
    keep, away = run(
        k_norm_back,
        where,
        steps,
        (*d_qkv, d_up, *qkv_w, *up_w),
        each(att, att, att, ff) + fixed(*qkv_w, *up_w),
        [shape((tokens, half_d))] * 2,
        each(half_d, half_d),
        flops=2 * tokens * width * (3 * att + ff),
    )
    away = swap(away, "tp", 1)
    part = (keep.astype(F32) + away.astype(F32)).astype(BF16).reshape(n_c, own_tok, half_d)
    d_norm = jnp.sum(dealt(part, "ctx").astype(F32), 0)
    qkv_grad = laid(grad_rows(normed, n_spec, d_qkv), 3)

    own = own_x.astype(F32)
    rest = lax.dynamic_slice_in_dim(x_other, c_at * own_tok, own_tok, 0).astype(F32)
    mean = (jnp.sum(own, -1, keepdims=True) + jnp.sum(rest, -1, keepdims=True)) / width
    own, rest = own - mean, rest - mean
    var = (jnp.sum(own * own, -1, keepdims=True) + jnp.sum(rest * rest, -1, keepdims=True)) / width
    inv = lax.rsqrt(var + EPS)
    own_hat = own * inv
    d_hat = d_norm * lax.dynamic_slice_in_dim(ln_gain, t_at * half_d, half_d, 0).astype(F32)
    sums = jnp.stack([jnp.sum(d_hat, -1), jnp.sum(d_hat * own_hat, -1)])
    sums = (sums + swap(sums, "tp", 1)) / width
    d_ln = inv * (d_hat - sums[0][:, None] - own_hat * sums[1][:, None])
    input_grad = d_ln + own_g.astype(F32)

    qkv_sum = jnp.sum(qkv_sums.reshape(rows_b, groups, 8, lanes)[:, :, :3], 0)
    early = jnp.concatenate(
        [up_sum.reshape(-1), jnp.swapaxes(qkv_sum, 0, 1).reshape(-1)]
    )
    early = jnp.sum(shown(early, ("fsdp", "ctx")).reshape(n_f, n_c, -1), 0)
    upb_grad = early[:, :ff].reshape(ff_half)
    bias_grad = jnp.moveaxis(early[:, ff:].reshape(n_c, 3, att), 0, 1).reshape(3, half_d)
    late = jnp.stack(
        [jnp.sum(d_norm * own_hat, 0), jnp.sum(d_norm, 0), jnp.sum(own_g.astype(F32), 0)]
    )
    late = jnp.sum(shown(late, ("fsdp", "ctx")), 0)
    return (
        block_out.reshape(l_dev, rows_b, half_d),
        input_grad.reshape(l_dev, rows_b, half_d),
        late[0],
        late[1],
        qkv_grad,
        bias_grad,
        out_weight_grad,
        up_grad,
        upb_grad,
        down_grad,
        late[2],
    )


def solution(mesh):
    return jax.shard_map(
        local,
        mesh=mesh,
        in_specs=(
            P("ctx", "fsdp", "tp"),
            P("ctx", "fsdp", "tp"),
            P("fsdp", None),
            P("fsdp", None),
            P(),
            P(),
            P(("fsdp", "ctx"), None, "tp"),
            P(None, "tp"),
            P(("fsdp", "ctx"), "tp"),
            P(("fsdp", "ctx"), "tp"),
            P("tp"),
            P(("fsdp", "ctx"), "tp"),
            P("tp"),
        ),
        out_specs=(
            P("ctx", "fsdp", "tp"),
            P("ctx", "fsdp", "tp"),
            P("tp"),
            P("tp"),
            P(("fsdp", "ctx"), None, "tp"),
            P(None, "tp"),
            P(("fsdp", "ctx"), "tp"),
            P(("fsdp", "ctx"), "tp"),
            P("tp"),
            P(("fsdp", "ctx"), "tp"),
            P("tp"),
        ),
        check_vma=False,
    )
```

```python
import functools
import math

import jax
import jax.numpy as jnp
from jax import lax
from jax.experimental import pallas as pl
from jax.experimental.pallas import tpu as pltpu
from jax.sharding import PartitionSpec as P


HD = 64
ROT = 32
EPS = 1e-05
NEVER = -1e30
BLOCK = 256
F32 = jnp.float32
BF16 = jnp.bfloat16


def run(kernel, where, grid, ins, in_specs, outs, out_specs, scratch=(), flops=0):
    moved = sum(math.prod(v.shape) * v.dtype.itemsize for v in (*ins, *outs))
    return pl.pallas_call(
        kernel,
        grid_spec=pltpu.PrefetchScalarGridSpec(
            num_scalar_prefetch=1,
            grid=grid,
            in_specs=in_specs,
            out_specs=out_specs,
            scratch_shapes=scratch,
        ),
        out_shape=outs,
        compiler_params=pltpu.CompilerParams(
            dimension_semantics=("arbitrary",) * len(grid), vmem_limit_bytes=56 << 20
        ),
        cost_estimate=pl.CostEstimate(flops=flops, bytes_accessed=moved, transcendentals=0),
    )(where, *ins)


def shape(dims, kind=BF16):
    return jax.ShapeDtypeStruct(dims, kind)


def whole_spec(value):
    return pl.BlockSpec(value.shape, lambda *_: (0,) * value.ndim)


def rows_spec(cols, block=BLOCK):
    return pl.BlockSpec((block, cols), lambda i, *_: (i, 0))


def dot(left, right, dims=((1,), (0,))):
    return lax.dot_general(left, right, (dims, ((), ())), preferred_element_type=F32)


def turn(value, cos_t, low_t, high_t, half):
    n = value.shape[-1]
    reps = n // cos_t.shape[-1]
    if reps > 1:
        cos_t, low_t, high_t = (jnp.concatenate([v] * reps, -1) for v in (cos_t, low_t, high_t))
    up = pltpu.roll(value, n - half, value.ndim - 1)
    down = pltpu.roll(value, half, value.ndim - 1)
    return value * cos_t + up * low_t + down * high_t


def k_qkv(at, x, gain, bias, w0, w1, w2, w3, qb, cos_t, low_t, high_t, normed, q, k, v):
    f_at = at[0]
    half = x.shape[3]
    width = 2 * half
    parts = [x[0, h].astype(F32) for h in range(2)]
    mean = sum(jnp.sum(p, -1, keepdims=True) for p in parts) / width
    parts = [p - mean for p in parts]
    var = sum(jnp.sum(p * p, -1, keepdims=True) for p in parts) / width
    inv = lax.rsqrt(var + EPS)
    for h, part in enumerate(parts):
        line = part * inv * gain[h].astype(F32) + bias[h].astype(F32)
        normed[:, h * half : (h + 1) * half] = line.astype(BF16)
    acc = qb[...]
    for n, w in enumerate((w0, w1, w2, w3)):
        rows = w.shape[0]
        at_col = pl.multiple_of((f_at ^ n) * rows, rows)
        acc = acc + dot(normed[:, pl.ds(at_col, rows)], w[...])
    att = q.shape[1]
    tables = (cos_t[...], low_t[...], high_t[...])
    q[...] = turn(acc[:, :att], *tables, ROT // 2).astype(BF16)
    k[...] = turn(acc[:, att : 2 * att], *tables, ROT // 2).astype(BF16)
    v[...] = acc[:, 2 * att :].astype(BF16)


def k_up(at, normed, w0, w1, w2, w3, ub, act, slope):
    f_at = at[0]
    acc = ub[...]
    for n, w in enumerate((w0, w1, w2, w3)):
        rows = w.shape[0]
        at_col = pl.multiple_of((f_at ^ n) * rows, rows)
        acc = acc + dot(normed[:, pl.ds(at_col, rows)], w[...])
    c0, c1 = 0.7978845608028654, 0.044715
    square = acc * acc
    bent = jnp.tanh(c0 * acc * (1.0 + c1 * square))
    act[...] = (0.5 * acc * (1.0 + bent)).astype(BF16)
    slope[...] = (
        0.5 * (1.0 + bent) + 0.5 * acc * (1.0 - bent * bent) * c0 * (1.0 + 3.0 * c1 * square)
    ).astype(BF16)


def head_masks(width):
    lane = lax.broadcasted_iota(jnp.int32, (1, width), 1)
    return [lane // HD == h for h in range(width // HD)]


def pair_mask(seg_col, seg_row, start, rows, keys):
    row = start + lax.broadcasted_iota(jnp.int32, (rows, keys), 0)
    col = lax.broadcasted_iota(jnp.int32, (rows, keys), 1)
    same = seg_col[0, pl.ds(start, rows), :] == seg_row[0, :, pl.ds(0, keys)]
    return jnp.where(same & (row >= col), 0.0, NEVER)


def k_attend(at, q, k, v, seg_col, seg_row, out, lse):
    length, width = q.shape[1:]
    rows = min(256, length)
    heads = head_masks(width)
    for i in range(length // rows):
        span, keys = pl.ds(i * rows, rows), (i + 1) * rows
        mask = pair_mask(seg_col, seg_row, i * rows, rows, keys)
        q_i, k_i, v_i = q[0, span, :], k[0, pl.ds(0, keys), :], v[0, pl.ds(0, keys), :]
        total = jnp.zeros((rows, width), F32)
        logs = jnp.zeros((rows, width), F32)
        for mine in heads:
            q_h = jnp.where(mine, q_i, 0) * jnp.asarray(1.0 / math.sqrt(HD), BF16)
            scores = dot(q_h, k_i, ((1,), (1,))) + mask
            top = jnp.max(scores, -1, keepdims=True)
            weights = jnp.exp(scores - top)
            mass = jnp.sum(weights, -1, keepdims=True)
            got = dot(weights.astype(BF16), v_i) / mass
            total = jnp.where(mine, got, total)
            logs = jnp.where(mine, top + jnp.log(mass), logs)
        out[0, span, :] = total.astype(BF16)
        lse[0, span, :] = logs


def k_attend_back(
    at, q, k, v, d_out, lse, seg_col, seg_row, cos_t, low_t, high_t, dq, dk, dv, sums, k_acc, v_acc
):
    length, width = q.shape[1:]
    rows = min(256, length)
    heads = head_masks(width)
    scale = jnp.asarray(1.0 / math.sqrt(HD), BF16)
    k_acc[...] = jnp.zeros_like(k_acc)
    v_acc[...] = jnp.zeros_like(v_acc)
    q_sum = jnp.zeros((1, width), F32)
    for i in range(length // rows):
        span, keys = pl.ds(i * rows, rows), (i + 1) * rows
        mask = pair_mask(seg_col, seg_row, i * rows, rows, keys)
        q_i, d_i = q[0, span, :], d_out[0, span, :]
        k_i, v_i = k[0, pl.ds(0, keys), :], v[0, pl.ds(0, keys), :]
        dq_i = jnp.zeros((rows, width), F32)
        dk_i = jnp.zeros((keys, width), F32)
        dv_i = jnp.zeros((keys, width), F32)
        for h, mine in enumerate(heads):
            q_h = jnp.where(mine, q_i, 0) * scale
            d_h = jnp.where(mine, d_i, 0)
            k_h = jnp.where(mine, k_i, 0) * scale
            scores = dot(q_h, k_i, ((1,), (1,))) + mask
            probs = jnp.exp(scores - lse[0, span, h * HD : h * HD + 1])
            d_prob = dot(d_h, v_i, ((1,), (1,)))
            delta = jnp.sum(probs * d_prob, -1, keepdims=True)
            d_score = (probs * (d_prob - delta)).astype(BF16)
            dq_i = dq_i + dot(d_score, k_h)
            dk_i = dk_i + dot(d_score, q_h, ((0,), (0,)))
            dv_i = dv_i + dot(probs.astype(BF16), d_h, ((0,), (0,)))
        k_acc[pl.ds(0, keys), :] += dk_i
        v_acc[pl.ds(0, keys), :] += dv_i
        tables = (cos_t[0, span, :], -low_t[0, span, :], -high_t[0, span, :])
        line = turn(dq_i, *tables, ROT // 2).astype(BF16)
        dq[0, span, :] = line
        q_sum = q_sum + jnp.sum(line.astype(F32), 0, keepdims=True)
    tables = (cos_t[0], -low_t[0], -high_t[0])
    line_k = turn(k_acc[...], *tables, ROT // 2).astype(BF16)
    line_v = v_acc[...].astype(BF16)
    dk[0] = line_k
    dv[0] = line_v
    sums[0, 0:1, :] = q_sum
    sums[0, 1:2, :] = jnp.sum(line_k.astype(F32), 0, keepdims=True)
    sums[0, 2:3, :] = jnp.sum(line_v.astype(F32), 0, keepdims=True)


def put_half(value, n, at, keep, away, halves):
    f_at, t_at = at[0], at[2]
    block = f_at ^ n
    cols = value.shape[1]
    here = pl.ds(pl.multiple_of((block % halves) * cols, cols), cols)
    own = block // halves == t_at

    @pl.when(own)
    def _():
        keep[:, here] = value.astype(keep.dtype)

    @pl.when(jnp.logical_not(own))
    def _():
        away[:, here] = value.astype(away.dtype)


def k_out(at, attn, act, w0, w1, w2, w3, keep, away):
    att = attn.shape[1]
    for n, w in enumerate((w0, w1, w2, w3)):
        term = dot(attn[...], w[:, :att], ((1,), (1,))) + dot(act[...], w[:, att:], ((1,), (1,)))
        put_half(term, n, at, keep, away, 2)


def k_norm_back(at, dq, dk, dv, d_up, a0, a1, a2, a3, w0, w1, w2, w3, keep, away):
    att = dq.shape[1]
    for n, (a, w) in enumerate(((a0, w0), (a1, w1), (a2, w2), (a3, w3))):
        term = dot(d_up[...], w[...], ((1,), (1,)))
        for p, d in enumerate((dq, dk, dv)):
            term = term + dot(d[...], a[:, p * att : (p + 1) * att], ((1,), (1,)))
        put_half(term, n, at, keep, away, 2)


def k_out_back(at, g, slope, w0, w1, w2, w3, d_att, d_up, sums):
    f_at = at[0]
    att = d_att.shape[1]
    acc = None
    for n, w in enumerate((w0, w1, w2, w3)):
        block = f_at ^ n
        rows = w.shape[0]
        cols = pl.ds(pl.multiple_of((block % 2) * rows, rows), rows)
        term = dot(g[0, block // 2, :, cols], w[...])
        acc = term if acc is None else acc + term
    d_att[...] = acc[:, :att].astype(BF16)
    line = (acc[:, att:] * slope[...].astype(F32)).astype(BF16)
    d_up[...] = line

    @pl.when(pl.program_id(0) == 0)
    def _():
        sums[...] = jnp.zeros_like(sums)

    sums[...] += jnp.sum(line.astype(F32), 0, keepdims=True)


def k_grad(at, left, *rest, adds):
    rights, out = rest[: -1 - adds], rest[-1]
    lhs = left[...]
    lhs = lhs.reshape(-1, lhs.shape[-1])
    col = 0
    for right in rights:
        n = right.shape[1]
        term = dot(lhs, right[...], ((0,), (0,)))
        if adds:
            term = term + rest[-2][0, :, col : col + n].astype(F32)
        out[0, :, col : col + n] = term.astype(out.dtype)
        col += n


def swap(value, axis, bit):
    return lax.ppermute(value, axis, [(i, i ^ bit) for i in range(lax.axis_size(axis))])


def dealt(chunks, axis):
    return lax.all_to_all(chunks, axis, 0, 0)


def shown(value, axis):
    axes = (axis,) if isinstance(axis, str) else axis
    n = math.prod(lax.axis_size(a) for a in axes)
    return dealt(jnp.broadcast_to(value[None], (n,) + value.shape), axis)


def row_of(block):
    n_c, n_t = lax.axis_size("ctx"), lax.axis_size("tp")
    c_at, t_at = lax.axis_index("ctx"), lax.axis_index("tp")
    tokens, half = block.shape
    if n_c != 4:
        mine = shown(block, "ctx")
        other = swap(mine, "tp", 1)
        first = t_at == 0
        return jnp.stack([jnp.where(first, mine, other), jnp.where(first, other, mine)], 1)
    out = jnp.zeros((n_c, n_t, tokens, half), block.dtype)

    def put(out, value, slot, t):
        return lax.dynamic_update_slice(out, value[None, None], (slot, t, 0, 0))

    right_side = c_at // 2
    pair = swap(block, "ctx", 1)
    mid1 = lax.ppermute(block, "ctx", [(1, 2), (2, 1)])
    mid2 = lax.ppermute(pair, "ctx", [(1, 2), (2, 1)])
    end1 = lax.ppermute(mid1, "ctx", [(1, 0), (2, 3)])
    end2 = lax.ppermute(mid2, "ctx", [(1, 0), (2, 3)])
    inner = (c_at == 1) | (c_at == 2)
    near = jnp.where(inner, mid1, end1)
    last = jnp.where(inner, mid2, end2)
    slots = (c_at, c_at ^ 1, 2 - right_side, 3 - 3 * right_side)
    for value, slot in zip((block, pair, near, last), slots):
        out = put(out, value, slot, t_at)
        out = put(out, swap(value, "tp", 1), slot, 1 - t_at)
    return out


def rotary_tables(pos, lanes):
    lane = jnp.arange(lanes, dtype=jnp.int32) % HD
    half = ROT // 2
    freqs = jnp.exp((lane % half).astype(F32) * (-2.0 * math.log(10000.0) / ROT))
    freqs = jnp.where(lane < ROT, freqs, 0.0)
    angles = pos.astype(F32)[:, None] * freqs[None, :]
    sines = jnp.sin(angles)
    return (
        jnp.cos(angles),
        jnp.where(lane < half, -sines, 0.0),
        jnp.where((lane >= half) & (lane < ROT), sines, 0.0),
    )


def local(
    hidden_in,
    out_grad,
    segment_ids,
    positions,
    ln_gain,
    ln_bias,
    w_qkv,
    qkv_bias,
    w_out,
    w_up,
    up_bias,
    w_down,
    out_bias,
):
    l_dev, rows_b, half_d = hidden_in.shape
    n_f, n_c, n_t = (lax.axis_size(a) for a in ("fsdp", "ctx", "tp"))
    assert n_f == 4 and n_t == 2
    width = half_d * n_t
    length = l_dev * n_c
    own_tok = l_dev * rows_b
    tokens = length * rows_b
    att = half_d // n_c
    ff_half = w_up.shape[1]
    ff = ff_half // n_c
    shard = w_up.shape[0]
    lanes = min(2 * HD, att)
    groups = att // lanes
    t_at, c_at, f_at = lax.axis_index("tp"), lax.axis_index("ctx"), lax.axis_index("fsdp")
    where = jnp.stack([f_at, c_at, t_at]).astype(jnp.int32)
    steps = (n_c,)
    piece = n_c * shard

    own_x = hidden_in.reshape(own_tok, half_d)
    own_g = out_grad.reshape(own_tok, half_d)

    def chunks_of(weight, cols):
        parts = weight.reshape(shard, -1, n_c, cols)
        return jnp.moveaxis(parts, 2, 0).reshape(n_c, shard, -1)

    def spread(chunks):
        mine = dealt(chunks, "ctx").reshape(piece, -1)
        across = swap(mine, "fsdp", 2)
        return (mine, swap(mine, "fsdp", 1), across, swap(across, "fsdp", 1))

    x_all = row_of(own_x)
    qkv_w = spread(chunks_of(w_qkv, att))
    up_w = spread(chunks_of(w_up, ff))
    od_w = spread(jnp.concatenate([chunks_of(w_out, att), chunks_of(w_down, ff)], 2))
    g_all = row_of(own_g)

    tables = rotary_tables(positions.T.reshape(tokens), lanes)
    qkv_b = lax.dynamic_slice_in_dim(qkv_bias, c_at * att, att, 1).astype(F32).reshape(1, -1)
    up_b = lax.dynamic_slice_in_dim(up_bias, c_at * ff, ff, 0).astype(F32).reshape(1, -1)
    gain2 = ln_gain.reshape(n_t, 1, half_d)
    bias2 = ln_bias.reshape(n_t, 1, half_d)

    def fixed(*values):
        return [whole_spec(v) for v in values]

    def each(*cols):
        return [rows_spec(c, own_tok) for c in cols]

    both = pl.BlockSpec((1, n_t, own_tok, half_d), lambda i, *_: (i, 0, 0, 0))
    normed, q, k, v = run(
        k_qkv,
        where,
        steps,
        (x_all, gain2, bias2, *qkv_w, qkv_b, *tables),
        [both] + fixed(gain2, bias2, *qkv_w, qkv_b) + each(lanes, lanes, lanes),
        [shape((tokens, width))] + [shape((tokens, att))] * 3,
        each(width, att, att, att),
        flops=2 * tokens * width * 3 * att,
    )

    def by_row(value):
        return jnp.moveaxis(value.reshape(length, rows_b, -1), 1, 0)

    def by_token(value):
        return jnp.moveaxis(value, 0, 1).reshape(tokens, -1)

    group = pl.BlockSpec((1, length, lanes), lambda r, h, *_: (r, 0, h))
    table = pl.BlockSpec((1, length, lanes), lambda r, h, *_: (r, 0, 0))
    seg_specs = [
        pl.BlockSpec((1, length, 1), lambda r, h, *_: (r, 0, 0)),
        pl.BlockSpec((1, 1, length), lambda r, h, *_: (r, 0, 0)),
    ]
    segs = (segment_ids[:, :, None], segment_ids[:, None, :])
    row_shape = (rows_b, length, att)
    pairs = rows_b * length * length * att
    q_r, k_r, v_r = by_row(q), by_row(k), by_row(v)
    attn_r, lse = run(
        k_attend,
        where,
        (rows_b, groups),
        (q_r, k_r, v_r, *segs),
        [group] * 3 + seg_specs,
        [shape(row_shape), shape(row_shape, F32)],
        [group] * 2,
        flops=4 * pairs,
    )
    attn = by_token(attn_r)

    act, slope = run(
        k_up,
        where,
        steps,
        (normed, *up_w, up_b),
        each(width) + fixed(*up_w, up_b),
        [shape((tokens, ff))] * 2,
        each(ff, ff),
        flops=2 * tokens * width * ff,
    )
    out_keep, out_away = run(
        k_out,
        where,
        steps,
        (attn, act, *od_w),
        each(att, ff) + fixed(*od_w),
        [shape((tokens, half_d))] * 2,
        each(half_d, half_d),
        flops=2 * tokens * width * (att + ff),
    )

    def token_sum(keep, away):
        came = swap(away, "tp", 1)
        part = (keep.astype(F32) + came.astype(F32)).astype(BF16)
        return jnp.sum(dealt(part.reshape(n_c, own_tok, half_d), "ctx").astype(F32), 0)

    branch = token_sum(out_keep, out_away)
    block_out = (own_x.astype(F32) + branch + out_bias.astype(F32)).astype(BF16)

    def grad_rows(left, left_spec, rights):
        cols = sum(v.shape[1] for v in rights)
        dims = (2, piece, cols)
        result = pl.BlockSpec((1, piece, cols), lambda i, *_: (i, 0, 0))
        flops = tokens * width * cols

        def half(parity, *came):
            return run(
                functools.partial(k_grad, adds=len(came)),
                where,
                (2,),
                (left, *rights, *came),
                [left_spec(parity)] + fixed(*rights) + [result] * len(came),
                [shape(dims)],
                [result],
                flops=flops,
            )[0]

        came = swap(half(1), "fsdp", 1)
        kept = half(0, came)
        x_at = f_at // 2
        away = lax.dynamic_index_in_dim(kept, 1 - x_at, 0, keepdims=False)
        came = swap(away, "fsdp", 2)
        own = lax.dynamic_index_in_dim(kept, x_at, 0, keepdims=False)
        total = (own.astype(F32) + came.astype(F32)).astype(BF16)
        return dealt(total.reshape(n_c, shard, cols), "ctx").astype(F32)

    def laid(value, parts):
        parted = value.reshape(n_c, shard, parts, -1)
        return jnp.moveaxis(parted, 0, 2).reshape(shard, parts, -1)

    def g_spec(parity):
        return pl.BlockSpec(
            (n_c, 1, own_tok, piece), lambda i, at: (0, i, 0, (at[0] + parity) % 2)
        )

    def n_spec(parity):
        return pl.BlockSpec((tokens, piece), lambda i, at: (0, 2 * i + (at[0] + parity) % 2))

    came = grad_rows(g_all, g_spec, (attn, act))
    out_weight_grad = laid(came[..., :att], 1).reshape(shard, half_d)
    down_grad = laid(came[..., att:], 1).reshape(shard, ff_half)

    d_att, d_up, up_sum = run(
        k_out_back,
        where,
        steps,
        (g_all, slope, *od_w),
        [both] + each(ff) + fixed(*od_w),
        [shape((tokens, att)), shape((tokens, ff)), shape((1, ff), F32)],
        each(att, ff) + [pl.BlockSpec((1, ff), lambda i, *_: (0, 0))],
        flops=2 * tokens * width * (att + ff),
    )
    came = grad_rows(normed, n_spec, (d_up,))
    up_grad = laid(came, 1).reshape(shard, ff_half)

    row_tables = [by_row(v) for v in tables]
    dq, dk, dv, qkv_sums = run(
        k_attend_back,
        where,
        (rows_b, groups),
        (q_r, k_r, v_r, by_row(d_att), lse, *segs, *row_tables),
        [group] * 5 + seg_specs + [table] * 3,
        [shape(row_shape)] * 3 + [shape((rows_b * groups, 8, lanes), F32)],
        [group] * 3
        + [pl.BlockSpec((1, 8, lanes), lambda r, h, *_: (r * groups + h, 0, 0))],
        [pltpu.VMEM((length, lanes), F32)] * 2,
        flops=10 * pairs,
    )
    d_qkv = tuple(by_token(d) for d in (dq, dk, dv))
    keep, away = run(
        k_norm_back,
        where,
        steps,
        (*d_qkv, d_up, *qkv_w, *up_w),
        each(att, att, att, ff) + fixed(*qkv_w, *up_w),
        [shape((tokens, half_d))] * 2,
        each(half_d, half_d),
        flops=2 * tokens * width * (3 * att + ff),
    )
    d_norm = token_sum(keep, away)
    qkv_grad = laid(grad_rows(normed, n_spec, d_qkv), 3)

    own = own_x.astype(F32)
    rest = lax.dynamic_slice(x_all, (c_at, 1 - t_at, 0, 0), (1, 1, own_tok, half_d))
    rest = rest.reshape(own_tok, half_d).astype(F32)
    mean = (jnp.sum(own, -1, keepdims=True) + jnp.sum(rest, -1, keepdims=True)) / width
    own, rest = own - mean, rest - mean
    var = (jnp.sum(own * own, -1, keepdims=True) + jnp.sum(rest * rest, -1, keepdims=True)) / width
    inv = lax.rsqrt(var + EPS)
    own_hat = own * inv
    d_hat = d_norm * lax.dynamic_slice_in_dim(ln_gain, t_at * half_d, half_d, 0).astype(F32)
    sums = jnp.stack([jnp.sum(d_hat, -1), jnp.sum(d_hat * own_hat, -1)])
    sums = (sums + swap(sums, "tp", 1)) / width
    d_ln = inv * (d_hat - sums[0][:, None] - own_hat * sums[1][:, None])
    input_grad = d_ln + own_g.astype(F32)

    qkv_sum = jnp.sum(qkv_sums.reshape(rows_b, groups, 8, lanes)[:, :, :3], 0)
    early = jnp.concatenate(
        [up_sum.reshape(-1), jnp.swapaxes(qkv_sum, 0, 1).reshape(-1)]
    )
    early = jnp.sum(shown(early, ("fsdp", "ctx")).reshape(n_f, n_c, -1), 0)
    upb_grad = early[:, :ff].reshape(ff_half)
    bias_grad = jnp.moveaxis(early[:, ff:].reshape(n_c, 3, att), 0, 1).reshape(3, half_d)
    late = jnp.stack(
        [jnp.sum(d_norm * own_hat, 0), jnp.sum(d_norm, 0), jnp.sum(own_g.astype(F32), 0)]
    )
    late = jnp.sum(shown(late, ("fsdp", "ctx")), 0)
    return (
        block_out.reshape(l_dev, rows_b, half_d),
        input_grad.reshape(l_dev, rows_b, half_d),
        late[0],
        late[1],
        qkv_grad,
        bias_grad,
        out_weight_grad,
        up_grad,
        upb_grad,
        down_grad,
        late[2],
    )


def solution(mesh):
    return jax.shard_map(
        local,
        mesh=mesh,
        in_specs=(
            P("ctx", "fsdp", "tp"),
            P("ctx", "fsdp", "tp"),
            P("fsdp", None),
            P("fsdp", None),
            P(),
            P(),
            P(("fsdp", "ctx"), None, "tp"),
            P(None, "tp"),
            P(("fsdp", "ctx"), "tp"),
            P(("fsdp", "ctx"), "tp"),
            P("tp"),
            P(("fsdp", "ctx"), "tp"),
            P("tp"),
        ),
        out_specs=(
            P("ctx", "fsdp", "tp"),
            P("ctx", "fsdp", "tp"),
            P("tp"),
            P("tp"),
            P(("fsdp", "ctx"), None, "tp"),
            P(None, "tp"),
            P(("fsdp", "ctx"), "tp"),
            P(("fsdp", "ctx"), "tp"),
            P("tp"),
            P(("fsdp", "ctx"), "tp"),
            P("tp"),
        ),
        check_vma=False,
    )
```
